128 devices in a mesh: grp: 2 (over core), ctx: 64 (over y, x, z).
Axes of the slice: x: 4, y: 4, z: 4, core: 2. Of those that a mesh axis runs over, the one named last changes fastest.
Arguments:
- queries: bfloat16 [98304, 32, 128], P(('grp', 'ctx')), may hold values from -6 to 6
- keys: bfloat16 [98304, 32, 128], P(('grp', 'ctx')), may hold values from -6 to 6
- values: bfloat16 [98304, 32, 128], P(('grp', 'ctx')), may hold values from -6 to 6
- norm_gain: float32 [4096], replicated, may hold values from 0.5 to 1.5
Outputs:
- attended: bfloat16 [98304, 32, 128], P(('grp', 'ctx'))
The draws below stay inside these ranges and needn't reach their ends.
All inputs are finite; a program needn't handle non-finite values.
Results may differ from the reference program's by a relative error of at most 0.0049.
Values sent between devices are 32-bit elements; how exact they have to be, the bound alone decides.
No kernel may reach another device: no remote copies, remote signals or barrier semaphores. Data moves between devices by JAX's collectives and lax.ppermute only.
A program may use at most 640 MiB of HBM per device.

```python
import jax
import jax.numpy as jnp
from jax import lax

HEADS = 32
HD = 128
BLOCK = 128
TOKENS = 98304


def shard_levels(stream_key, extent, shards, least, largest):
    level, own = 1.0, jax.random.fold_in(stream_key, 6)
    for dim, blocks in shards:
        heights = jnp.exp(jax.random.uniform(jax.random.fold_in(own, dim), (blocks,), jnp.float32, least / len(shards), largest / len(shards)))
        level = level * jnp.repeat(heights, extent[dim] // blocks).reshape([-1 if axis == dim else 1 for axis in range(len(extent))])
    return level


def noise(key, extent, width, bound, cuts=(), kind=jnp.bfloat16):
    array = width * jax.random.normal(key, extent, jnp.float32)
    if cuts:
        array = array * shard_levels(key, extent, cuts, -0.22, 0.18)
    return jnp.clip(array, -bound, bound).astype(kind)


def setup_inputs(seed: int = 0) -> dict:
    key_list = jax.random.split(jax.random.key(seed), 5)
    queries = noise(key_list[0], (TOKENS, HEADS, HD), 1.0, 6.0, ((0, 128),))
    keys = noise(key_list[1], (TOKENS, HEADS, HD), 1.0, 6.0, ((0, 128),))
    values = noise(key_list[2], (TOKENS, HEADS, HD), 1.0, 6.0, ((0, 128),))
    norm_gain = jnp.clip(1.0 + 0.1 * jax.random.normal(key_list[3], (HEADS * HD,), jnp.float32), 0.5, 1.5)
    return dict(queries=queries, keys=keys, values=values, norm_gain=norm_gain)


def reference(queries, keys, values, norm_gain):
    count = TOKENS // BLOCK
    qs = queries.reshape(count, BLOCK, HEADS, HD)
    ks = keys.reshape(count, BLOCK, HEADS, HD)
    vs = values.reshape(count, BLOCK, HEADS, HD)
    rows = jnp.arange(BLOCK)
    causal = rows[:, None] >= rows[None, :]
    gain = norm_gain.reshape(HEADS, HD)

    def step(state, pieces):
        qc, kc, vc = pieces
        qf = qc.astype(jnp.float32)
        kf = kc.astype(jnp.float32)
        vf = vc.astype(jnp.float32)
        scores = jnp.einsum('qhd,khd->hqk', qf, kf)
        scores = jnp.where(causal[None], scores, 0.0).astype(jnp.bfloat16)
        intra = jnp.einsum('hqk,khd->qhd', scores.astype(jnp.float32), vf)
        rounded = state.astype(jnp.bfloat16).astype(jnp.float32)
        inter = jnp.einsum('qhd,hde->qhe', qf, rounded)
        grown = state + jnp.einsum('khd,khe->hde', kf, vf)
        mixed = intra + inter
        power = lax.optimization_barrier(jnp.mean(mixed * mixed, axis=(1, 2), keepdims=True))
        normed = mixed * lax.rsqrt(power + 1e-06) * gain[None]
        return (grown, normed.astype(jnp.bfloat16))
    start = jnp.zeros((HEADS, HD, HD), jnp.float32)
    final_state, outputs = lax.scan(step, start, (qs, ks, vs))
    return outputs.reshape(TOKENS, HEADS, HD)
```

```python
import jax
import jax.numpy as jnp
from jax import lax
from jax.experimental import pallas as pl
from jax.experimental.pallas import tpu as pltpu
from jax.sharding import PartitionSpec as P

BLOCK = 128
HD = 128
PAIR = 2 * HD
MIB = 1 << 20
VMEM = pl.BlockSpec(memory_space=pltpu.VMEM)
HBM = pl.BlockSpec(memory_space=pltpu.HBM)


def in_vmem(x):
    return pltpu.with_memory_space_constraint(x, pltpu.VMEM)


def in_hbm(x):
    return pltpu.with_memory_space_constraint(x, pltpu.HBM)


def params(mib):
    return pltpu.CompilerParams(vmem_limit_bytes=mib * MIB)


def dot(a, b, dims):
    return lax.dot_general(a, b, (dims, ((), ())), preferred_element_type=jnp.float32)


def parity(rows, width):
    return lax.rem(lax.broadcasted_iota(jnp.int32, (rows, width), 0), 2)


def by_head(x, par):
    zero = jnp.zeros_like(x)
    return jnp.concatenate([jnp.where(par == 0, x, zero), jnp.where(par == 1, x, zero)], axis=1)


def pair_copies(ins, outs, sem, first, pairs):
    return [
        pltpu.make_async_copy(src.at[:, f + m], dst.at[m], sem.at[i, m])
        for i, (src, dst, f, n) in enumerate(zip(ins, outs, first, pairs))
        for m in range(n)
    ]


def paired(x):
    return x.reshape(x.shape[0], -1, HD)


def relay(arrays, first, pairs):
    n, tokens = len(arrays), arrays[0].shape[0]

    def body(*refs):
        copies = pair_copies(refs[:n], refs[n : 2 * n], refs[2 * n], first, pairs)
        for c in copies:
            c.start()
        for c in copies:
            c.wait()

    return pl.pallas_call(
        body,
        in_specs=[HBM] * n,
        out_specs=[VMEM] * n,
        out_shape=[pltpu.VMEM((p, tokens, 2, HD), jnp.bfloat16) for p in pairs],
        scratch_shapes=[pltpu.SemaphoreType.DMA((n, max(pairs)))],
        compiler_params=params(1),
        name="relay",
    )(*[in_hbm(a) for a in arrays])


def totals(k, v, arrays, first, pairs):
    n, rows = len(arrays), k.shape[1]
    tokens = rows // 2

    def body(*refs):
        k_ref, v_ref, ins = refs[0], refs[1], refs[2 : 2 + n]
        o_ref, outs, sem = refs[2 + n], refs[3 + n : 3 + 2 * n], refs[3 + 2 * n]
        copies = pair_copies(ins, outs, sem, first, pairs)
        for c in copies:
            c.start()

        def step(m, carry):
            s = dot(k_ref[m], by_head(v_ref[m], parity(rows, HD)), ((0,), (0,)))
            o_ref[2 * m] = s[:, :HD]
            o_ref[2 * m + 1] = s[:, HD:]
            return carry

        lax.fori_loop(0, k_ref.shape[0], step, 0)
        for c in copies:
            c.wait()

    return pl.pallas_call(
        body,
        in_specs=[VMEM, VMEM] + [HBM] * n,
        out_specs=[VMEM] + [VMEM] * n,
        out_shape=[jax.ShapeDtypeStruct((2 * k.shape[0], HD, HD), jnp.float32)]
        + [pltpu.VMEM((p, tokens, 2, HD), jnp.bfloat16) for p in pairs],
        scratch_shapes=[pltpu.SemaphoreType.DMA((n, max(pairs)))],
        compiler_params=params(8),
        name="totals",
    )(in_vmem(k), in_vmem(v), *[in_hbm(a) for a in arrays])


def local(q, k, v):
    pairs, rows, _ = q.shape
    blocks = rows // (2 * BLOCK)

    def body(q_ref, k_ref, v_ref, o_ref, mask):
        i = lax.broadcasted_iota(jnp.int32, (PAIR, PAIR), 0)
        j = lax.broadcasted_iota(jnp.int32, (PAIR, PAIR), 1)
        seen = (i >= j) & (lax.rem(i, 2) == lax.rem(j, 2))
        mask[...] = jnp.where(seen, 1.0, 0.0).astype(jnp.bfloat16)
        par = parity(PAIR, HD)

        def step(m, carry):
            state = jnp.zeros((HD, PAIR), jnp.float32)
            for c in range(blocks):
                at = pl.ds(c * PAIR, PAIR)
                q_c, k_c, v_c = q_ref[m, at], k_ref[m, at], v_ref[m, at]
                scores = dot(q_c, k_c, ((1,), (1,))).astype(jnp.bfloat16) * mask[...]
                mixed = dot(scores, v_c, ((1,), (0,)))
                if c > 0:
                    held = state.astype(jnp.bfloat16)
                    held = jnp.concatenate([held[:, :HD], held[:, HD:]], axis=0)
                    mixed += dot(by_head(q_c, par), held, ((1,), (0,)))
                o_ref[m, at] = mixed
                if c < blocks - 1:
                    state += dot(k_c, by_head(v_c, par), ((0,), (0,)))
            return carry

        lax.fori_loop(0, pairs, step, 0)

    return pl.pallas_call(
        body,
        in_specs=[VMEM] * 3,
        out_specs=VMEM,
        out_shape=pltpu.VMEM((pairs, rows, HD), jnp.float32),
        scratch_shapes=[pltpu.VMEM((PAIR, PAIR), jnp.bfloat16)],
        compiler_params=params(8),
        name="local",
    )(in_vmem(q), in_vmem(k), in_vmem(v))


def scan(parts):
    def body(x_ref, o_ref):
        def step(i, carry):
            o_ref[i] = carry
            return carry + x_ref[i]

        lax.fori_loop(0, x_ref.shape[0], step, jnp.zeros(x_ref.shape[1:], jnp.float32), unroll=8)

    return pl.pallas_call(
        body,
        in_specs=[VMEM],
        out_specs=VMEM,
        out_shape=jax.ShapeDtypeStruct(parts.shape, jnp.float32),
        compiler_params=params(8),
        name="scan",
    )(parts)


def with_prefix(q, prefix, mixed):
    pairs, rows, _ = q.shape

    def body(q_ref, p_ref, x_ref, o_ref, power):
        par = parity(PAIR, HD)

        def step(c, carry):
            at = pl.ds(pl.multiple_of(c * PAIR, PAIR), PAIR)
            total = jnp.zeros((PAIR, HD), jnp.float32)
            for m in range(pairs):
                held = p_ref[2 * m : 2 * m + 2].reshape(PAIR, HD).astype(jnp.bfloat16)
                x = x_ref[m, at] + dot(by_head(q_ref[m, at], par), held, ((1,), (0,)))
                o_ref[m, at] = x
                total += x * x
            power[at] = total
            return carry

        lax.fori_loop(0, rows // PAIR, step, 0)

    return pl.pallas_call(
        body,
        in_specs=[VMEM] * 3,
        out_specs=[VMEM] * 2,
        out_shape=[pltpu.VMEM(mixed.shape, jnp.float32), pltpu.VMEM((rows, HD), jnp.float32)],
        input_output_aliases={2: 0},
        compiler_params=params(8),
        name="with_prefix",
    )(in_vmem(q), prefix, in_vmem(mixed))


def normed(q, prefix, mixed, done, power, gain):
    pairs, rows, _ = q.shape
    entries = 2 * HD * (pairs + done.shape[0])

    def body(q_ref, p_ref, x_ref, d_ref, power_ref, g_ref, o_ref, kept):
        par = parity(PAIR, HD)

        def step(c, carry):
            at = pl.ds(pl.multiple_of(c * PAIR, PAIR), PAIR)
            total = power_ref[at]
            for m in range(pairs):
                held = p_ref[2 * m : 2 * m + 2].reshape(PAIR, HD).astype(jnp.bfloat16)
                x = x_ref[m, at] + dot(by_head(q_ref[m, at], par), held, ((1,), (0,)))
                kept[m] = x
                total += x * x
            both = total + jnp.where(par == 0, pltpu.roll(total, PAIR - 1, 0), pltpu.roll(total, 1, 0))
            mean = jnp.sum(both, axis=1, keepdims=True) / entries
            scale = jnp.broadcast_to(lax.rsqrt(mean + 1e-06), (PAIR, HD))
            for m in range(done.shape[0]):
                x = (d_ref[m, at] * scale).reshape(PAIR // 8, 8, HD) * g_ref[m][None]
                o_ref[m, at] = x.reshape(PAIR, HD).astype(jnp.bfloat16)
            for m in range(pairs):
                x = (kept[m] * scale).reshape(PAIR // 8, 8, HD) * g_ref[done.shape[0] + m][None]
                o_ref[done.shape[0] + m, at] = x.reshape(PAIR, HD).astype(jnp.bfloat16)
            return carry

        lax.fori_loop(0, rows // PAIR, step, 0)

    return pl.pallas_call(
        body,
        in_specs=[VMEM] * 6,
        out_specs=VMEM,
        out_shape=pltpu.VMEM((pairs + done.shape[0], rows, HD), jnp.bfloat16),
        scratch_shapes=[pltpu.VMEM((pairs, PAIR, HD), jnp.float32)],
        compiler_params=params(8),
        name="normed",
    )(in_vmem(q), prefix, in_vmem(mixed), in_vmem(done), in_vmem(power), gain)


def relay_out(x):
    pairs, tokens = x.shape[:2]

    def body(x_ref, o_ref, sem):
        copies = [pltpu.make_async_copy(x_ref.at[m], o_ref.at[:, m], sem.at[m]) for m in range(pairs)]
        for c in copies:
            c.start()
        for c in copies:
            c.wait()

    return pl.pallas_call(
        body,
        in_specs=[VMEM],
        out_specs=HBM,
        out_shape=pltpu.HBM((tokens, pairs, 2, HD), jnp.bfloat16),
        scratch_shapes=[pltpu.SemaphoreType.DMA((pairs,))],
        compiler_params=params(1),
        name="relay_out",
    )(in_vmem(x))


def after(first, then):
    return lax.optimization_barrier((first, then))[1]


AXES = ("grp", "ctx")


def exchange(x):
    n = lax.axis_size("grp") * lax.axis_size("ctx")
    return lax.all_to_all(x.reshape(n, -1, HD), AXES, 0, 0)


def per_device(queries, keys, values, norm_gain):
    tokens, heads, width = queries.shape
    pairs = heads // 2
    half = pairs // 2
    q4, k4, v4 = (x.reshape(tokens, pairs, 2, width) for x in (queries, keys, values))
    gain = jnp.tile(norm_gain.reshape(pairs, 2, width), (1, 4, 1))

    ka, va = map(paired, relay([k4, v4], (0, 0), (half, half)))
    ta, kb, vb = totals(ka, va, [k4, v4], (half, half), (half, half))
    kb, vb = paired(kb), paired(vb)
    ga = exchange(ta)
    tb, qa, qb = totals(kb, vb, [q4, q4], (0, half), (half, half))
    qa, qb = paired(qa), paired(qb)
    gb = exchange(tb)
    xa = local(qa, ka, va)
    pa = exchange(scan(ga)).reshape(heads // 2, width, width)
    xb = local(qb, kb, vb)
    pb = exchange(scan(gb)).reshape(heads // 2, width, width)
    done, power = with_prefix(qa, pa, xa)
    out = normed(qb, pb, xb, done, power, gain)
    out = relay_out(out.reshape(pairs, tokens, 2, width))
    return out.reshape(tokens, heads, width)


def solution(mesh):
    spec = P(("grp", "ctx"), None, None)
    return jax.shard_map(
        per_device, mesh=mesh, in_specs=(spec, spec, spec, P()), out_specs=spec, check_vma=False
    )
```

```python
import jax
import jax.numpy as jnp
from jax import lax
from jax.experimental import pallas as pl
from jax.experimental.pallas import tpu as pltpu
from jax.sharding import PartitionSpec as P

BLOCK = 128
HD = 128
PAIR = 2 * HD
SIDE = 4
MIB = 1 << 20
VMEM = pl.BlockSpec(memory_space=pltpu.VMEM)
SMEM = pl.BlockSpec(memory_space=pltpu.SMEM)
HBM = pl.BlockSpec(memory_space=pltpu.HBM)


def in_vmem(x):
    return pltpu.with_memory_space_constraint(x, pltpu.VMEM)


def in_hbm(x):
    return pltpu.with_memory_space_constraint(x, pltpu.HBM)


def params(mib):
    return pltpu.CompilerParams(vmem_limit_bytes=mib * MIB)


def cost(us):
    return pl.CostEstimate(flops=int(us * 1e9), bytes_accessed=int(us * 3e6), transcendentals=0)


def f32(*shape):
    return pltpu.VMEM(shape, jnp.float32)


def bf16(*shape):
    return pltpu.VMEM(shape, jnp.bfloat16)


def dot(a, b, dims):
    return lax.dot_general(a, b, (dims, ((), ())), preferred_element_type=jnp.float32)


def parity(rows, width):
    return lax.rem(lax.broadcasted_iota(jnp.int32, (rows, width), 0), 2)


def by_head(x, par):
    zero = jnp.zeros_like(x)
    return jnp.concatenate([jnp.where(par == 0, x, zero), jnp.where(par == 1, x, zero)], axis=1)


def pair_copies(ins, outs, sem, first, pairs):
    return [
        pltpu.make_async_copy(src.at[:, f + m], dst.at[m], sem.at[i, m])
        for i, (src, dst, f, n) in enumerate(zip(ins, outs, first, pairs))
        for m in range(n)
    ]


def paired(x):
    return x.reshape(x.shape[0], -1, HD)


def relay(arrays, first, pairs):
    n, tokens = len(arrays), arrays[0].shape[0]

    def body(*refs):
        copies = pair_copies(refs[:n], refs[n : 2 * n], refs[2 * n], first, pairs)
        for c in copies:
            c.start()
        for c in copies:
            c.wait()

    return pl.pallas_call(
        body,
        in_specs=[HBM] * n,
        out_specs=[VMEM] * n,
        out_shape=[bf16(p, tokens, 2, HD) for p in pairs],
        scratch_shapes=[pltpu.SemaphoreType.DMA((n, max(pairs)))],
        compiler_params=params(1),
        cost_estimate=cost(3),
        name="relay",
    )(*[in_hbm(a) for a in arrays])


def totals(at, k, v, arrays, first, pairs):
    n, rows = len(arrays), k.shape[1]
    tokens = rows // 2
    part = k.shape[0] // SIDE

    def body(at_ref, k_ref, v_ref, *refs):
        ins, outs, gets, sem = refs[:n], refs[n : n + SIDE], refs[n + SIDE : -1], refs[-1]
        copies = pair_copies(ins, gets, sem, first, pairs)
        for c in copies:
            c.start()
        for d in range(SIDE):
            own = lax.rem(at_ref[0] + d, SIDE) * part

            def step(i, carry, d=d, own=own):
                s = dot(k_ref[own + i], by_head(v_ref[own + i], parity(rows, HD)), ((0,), (0,)))
                outs[d][2 * i] = s[:, :HD]
                outs[d][2 * i + 1] = s[:, HD:]
                return carry

            lax.fori_loop(0, part, step, 0)
        for c in copies:
            c.wait()

    return pl.pallas_call(
        body,
        in_specs=[SMEM, VMEM, VMEM] + [HBM] * n,
        out_specs=[VMEM] * (SIDE + n),
        out_shape=[f32(2 * part, HD, HD)] * SIDE + [bf16(p, tokens, 2, HD) for p in pairs],
        scratch_shapes=[pltpu.SemaphoreType.DMA((n, max(pairs)))],
        compiler_params=params(4),
        cost_estimate=cost(4),
        name="totals",
    )(at, in_vmem(k), in_vmem(v), *[in_hbm(a) for a in arrays])


def local(q, k, v):
    pairs, rows, _ = q.shape
    blocks = rows // PAIR

    def body(q_ref, k_ref, v_ref, o_ref, s_ref, mask):
        i = lax.broadcasted_iota(jnp.int32, (PAIR, PAIR), 0)
        j = lax.broadcasted_iota(jnp.int32, (PAIR, PAIR), 1)
        seen = (i >= j) & (lax.rem(i, 2) == lax.rem(j, 2))
        mask[...] = jnp.where(seen, 1.0, 0.0).astype(jnp.bfloat16)
        par = parity(PAIR, HD)

        def step(m, carry):
            state = None
            for c in range(blocks):
                at = pl.ds(c * PAIR, PAIR)
                q_c, k_c, v_c = q_ref[m, at], k_ref[m, at], v_ref[m, at]
                scores = dot(q_c, k_c, ((1,), (1,))).astype(jnp.bfloat16) * mask[...]
                o_ref[m, at] = dot(scores, v_c, ((1,), (0,)))
                if c < blocks - 1:
                    piece = dot(k_c, by_head(v_c, par), ((0,), (0,)))
                    state = piece if state is None else state + piece
                    s_ref[m, c, :HD] = state[:, :HD]
                    s_ref[m, c, HD:] = state[:, HD:]
            return carry

        lax.fori_loop(0, pairs, step, 0)

    return pl.pallas_call(
        body,
        in_specs=[VMEM] * 3,
        out_specs=[VMEM] * 2,
        out_shape=[f32(pairs, rows, HD), f32(pairs, blocks - 1, PAIR, HD)],
        scratch_shapes=[pltpu.VMEM((PAIR, PAIR), jnp.bfloat16)],
        compiler_params=params(4),
        cost_estimate=cost(9),
        name="local",
    )(in_vmem(q), in_vmem(k), in_vmem(v))


def added(parts):
    return (parts[0] + parts[1]) + (parts[2] + parts[3])


def before(at, axis, d, parts):
    here = lax.rem(at[axis] + d, SIDE)
    total = None
    for e, x in enumerate(parts):
        sender = lax.rem(at[axis] + (SIDE - e), SIDE)
        x = jnp.where(sender < here, x, 0.0)
        total = x if total is None else total + x
    return total


def small(body, name, shapes, at, arrays):
    return pl.pallas_call(
        body,
        in_specs=[SMEM] + [VMEM] * len(arrays),
        out_specs=[VMEM] * len(shapes),
        out_shape=[f32(*s) for s in shapes],
        compiler_params=params(4),
        cost_estimate=cost(0.7),
        name=name,
    )(at, *[in_vmem(a) for a in arrays])


def up_z(at, parts):
    rows = parts[0].shape[0] * HD // SIDE
    parts = [p.reshape(SIDE, rows, HD) for p in parts]

    def body(at_ref, *refs):
        for d in range(SIDE):
            own = lax.rem(at_ref[1] + d, SIDE)
            refs[SIDE + d][...] = added([r[own] for r in refs[:SIDE]])

    return small(body, "up_z", [(rows, HD)] * SIDE, at, parts)


def up_x(at, parts):
    def body(at_ref, *refs):
        refs[SIDE][...] = added([r[...] for r in refs[:SIDE]])

    return small(body, "up_x", [parts[0].shape], at, parts)[0]


def over_y(at, parts):
    def body(at_ref, *refs):
        got = [r[...] for r in refs[:SIDE]]
        refs[SIDE][...] = before(at_ref, 2, 0, got)
        refs[SIDE + 1][...] = added(got)

    return small(body, "over_y", [parts[0].shape] * 2, at, parts)


def down_x(at, parts, carry, group):
    def body(at_ref, *refs):
        got = [r[...] for r in refs[:SIDE]]
        held = refs[SIDE][...] + refs[SIDE + 1][...]
        for d in range(SIDE):
            refs[SIDE + 2 + d][...] = held + before(at_ref, 1, d, got)

    return small(body, "down_x", [parts[0].shape] * SIDE, at, [*parts, carry, group])


def down_z(at, parts, carries):
    heads = parts[0].shape[0]
    rows = heads * HD // SIDE
    parts = [p.reshape(SIDE, rows, HD) for p in parts]

    def body(at_ref, *refs):
        for e in range(SIDE):
            own = lax.rem(at_ref[1] + (SIDE - e), SIDE)
            got = [r[own] for r in refs[:SIDE]]
            held = refs[SIDE + e][...]
            for d in range(SIDE):
                refs[2 * SIDE + d][own] = held + before(at_ref, 0, d, got)

    outs = small(body, "down_z", [(SIDE, rows, HD)] * SIDE, at, [*parts, *carries])
    return [o.reshape(heads, HD, HD) for o in outs]


def with_state(q_ref, x_ref, s_ref, held, m, c, par):
    at = pl.ds(pl.multiple_of(c * PAIR, PAIR), PAIR)
    kept = s_ref[m, jnp.maximum(c - 1, 0)]
    state = (held + jnp.where(c > 0, kept, 0.0)).astype(jnp.bfloat16)
    return x_ref[m, at] + dot(by_head(q_ref[m, at], par), state, ((1,), (0,)))


def with_prefix(at, q, prefix, mixed, states):
    pairs, rows, _ = q.shape
    part = pairs // SIDE

    def body(at_ref, q_ref, x_ref, s_ref, *refs):
        p_refs, o_ref, power = refs[:SIDE], refs[SIDE], refs[SIDE + 1]
        par = parity(PAIR, HD)

        def step(c, carry):
            total = jnp.zeros((PAIR, HD), jnp.float32)
            for d in range(SIDE):
                own = lax.rem(at_ref[0] + (SIDE - d), SIDE) * part
                for i in range(part):
                    held = p_refs[d][2 * i : 2 * i + 2].reshape(PAIR, HD)
                    x = with_state(q_ref, x_ref, s_ref, held, own + i, c, par)
                    o_ref[own + i, pl.ds(pl.multiple_of(c * PAIR, PAIR), PAIR)] = x
                    total += x * x
            power[pl.ds(pl.multiple_of(c * PAIR, PAIR), PAIR)] = total
            return carry

        lax.fori_loop(0, rows // PAIR, step, 0)

    return pl.pallas_call(
        body,
        in_specs=[SMEM] + [VMEM] * (3 + SIDE),
        out_specs=[VMEM] * 2,
        out_shape=[f32(*mixed.shape), f32(rows, HD)],
        input_output_aliases={2: 0},
        compiler_params=params(4),
        cost_estimate=cost(4),
        name="with_prefix",
    )(at, in_vmem(q), in_vmem(mixed), in_vmem(states), *map(in_vmem, prefix))


def normed(at, q, prefix, mixed, states, done, power, gain):
    pairs, rows, _ = q.shape
    part, other = pairs // SIDE, done.shape[0]
    entries = 2 * HD * (pairs + other)

    def body(at_ref, q_ref, x_ref, s_ref, d_ref, power_ref, g_ref, *refs):
        p_refs, o_ref, kept = refs[:SIDE], refs[SIDE], refs[SIDE + 1]
        par = parity(PAIR, HD)

        def step(c, carry):
            rows_c = pl.ds(pl.multiple_of(c * PAIR, PAIR), PAIR)
            total = power_ref[rows_c]
            for d in range(SIDE):
                own = lax.rem(at_ref[0] + (SIDE - d), SIDE) * part
                for i in range(part):
                    held = p_refs[d][2 * i : 2 * i + 2].reshape(PAIR, HD)
                    x = with_state(q_ref, x_ref, s_ref, held, own + i, c, par)
                    kept[own + i] = x
                    total += x * x
            both = total + jnp.where(par == 0, pltpu.roll(total, PAIR - 1, 0), pltpu.roll(total, 1, 0))
            mean = jnp.sum(both, axis=1, keepdims=True) / entries
            scale = jnp.broadcast_to(lax.rsqrt(mean + 1e-06), (PAIR, HD))
            for m in range(other + pairs):
                x = d_ref[m, rows_c] if m < other else kept[m - other]
                x = (x * scale).reshape(PAIR // 8, 8, HD) * g_ref[m][None]
                o_ref[m, rows_c] = x.reshape(PAIR, HD).astype(jnp.bfloat16)
            return carry

        lax.fori_loop(0, rows // PAIR, step, 0)

    return pl.pallas_call(
        body,
        in_specs=[SMEM] + [VMEM] * (6 + SIDE),
        out_specs=VMEM,
        out_shape=bf16(pairs + other, rows, HD),
        scratch_shapes=[pltpu.VMEM((pairs, PAIR, HD), jnp.float32)],
        compiler_params=params(4),
        cost_estimate=cost(6),
        name="normed",
    )(at, *map(in_vmem, (q, mixed, states, done, power, gain, *prefix)))


def relay_out(x):
    pairs, tokens = x.shape[:2]

    def body(x_ref, o_ref, sem):
        copies = [pltpu.make_async_copy(x_ref.at[m], o_ref.at[:, m], sem.at[m]) for m in range(pairs)]
        for c in copies:
            c.start()
        for c in copies:
            c.wait()

    return pl.pallas_call(
        body,
        in_specs=[VMEM],
        out_specs=HBM,
        out_shape=pltpu.HBM((tokens, pairs, 2, HD), jnp.bfloat16),
        scratch_shapes=[pltpu.SemaphoreType.DMA((pairs,))],
        compiler_params=params(1),
        cost_estimate=cost(3),
        name="relay_out",
    )(in_vmem(x))


def shifted(dy, dx, dz):
    def to(i):
        y, x, z = i // SIDE**2, i // SIDE % SIDE, i % SIDE
        return ((y + dy) % SIDE * SIDE + (x + dx) % SIDE) * SIDE + (z + dz) % SIDE

    return [(i, to(i)) for i in range(SIDE**3)]


def sent(parts, axis):
    steps = [shifted(*[d if a == axis else 0 for a in (2, 1, 0)]) for d in range(SIDE)]
    return [parts[0]] + [lax.ppermute(parts[d], "ctx", steps[d]) for d in range(1, SIDE)]


def prefixes(at, parts):
    z_parts = sent(parts, 0)
    x_parts = sent(up_z(at, z_parts), 1)
    total = up_x(at, x_parts)
    y_parts = sent([total] * SIDE, 2)
    carry, group = over_y(at, y_parts)
    group = lax.ppermute(group, "grp", [(0, 1)])
    carries = sent(down_x(at, x_parts, carry, group), 1)
    return sent(down_z(at, z_parts, carries), 0)


def per_device(queries, keys, values, norm_gain):
    tokens, heads, width = queries.shape
    pairs = heads // 2
    half = pairs // 2
    q4, k4, v4 = (x.reshape(tokens, pairs, 2, width) for x in (queries, keys, values))
    gain = jnp.tile(norm_gain.reshape(pairs, 2, width), (1, 4, 1))
    ctx = lax.axis_index("ctx")
    at = jnp.stack([ctx % SIDE, ctx // SIDE % SIDE, ctx // SIDE**2]).astype(jnp.int32)

    ka, va = map(paired, relay([k4, v4], (0, 0), (half, half)))
    *ta, kb, vb = totals(at, ka, va, [k4, v4], (half, half), (half, half))
    kb, vb = paired(kb), paired(vb)
    *tb, qa, qb = totals(at, kb, vb, [q4, q4], (0, half), (half, half))
    qa, qb = paired(qa), paired(qb)
    pa = prefixes(at, ta)
    pb = prefixes(at, tb)
    xa, sa = local(qa, ka, va)
    xb, sb = local(qb, kb, vb)
    done, power = with_prefix(at, qa, pa, xa, sa)
    out = normed(at, qb, pb, xb, sb, done, power, gain)
    out = relay_out(out.reshape(pairs, tokens, 2, width))
    return out.reshape(tokens, heads, width)


def solution(mesh):
    spec = P(("grp", "ctx"), None, None)
    return jax.shard_map(
        per_device, mesh=mesh, in_specs=(spec, spec, spec, P()), out_specs=spec, check_vma=False
    )
```

```python
import jax
import jax.numpy as jnp
from jax import lax
from jax.experimental import pallas as pl
from jax.experimental.pallas import tpu as pltpu
from jax.sharding import PartitionSpec as P


HD = 128
PAIR = 2 * HD
MIB = 1 << 20
VMEM = pl.BlockSpec(memory_space=pltpu.VMEM)
HBM = pl.BlockSpec(memory_space=pltpu.HBM)
AXES = ("grp", "ctx")


def in_vmem(x):
    return pltpu.with_memory_space_constraint(x, pltpu.VMEM)


def in_hbm(x):
    return pltpu.with_memory_space_constraint(x, pltpu.HBM)


def params(mib):
    return pltpu.CompilerParams(vmem_limit_bytes=mib * MIB)


def cost(us):
    return pl.CostEstimate(flops=int(us * 1e9), bytes_accessed=int(us * 3e6), transcendentals=0)


def dot(a, b, dims):
    return lax.dot_general(a, b, (dims, ((), ())), preferred_element_type=jnp.float32)


def parity(rows, width):
    return lax.rem(lax.broadcasted_iota(jnp.int32, (rows, width), 0), 2)


def by_head(x):
    odd = parity(16, HD).astype(jnp.bfloat16)
    tiles = x.reshape(-1, 16, HD)
    halves = [(tiles * m[None]).reshape(x.shape) for m in (1 - odd, odd)]
    return jnp.concatenate(halves, axis=1)


def paired(x):
    return x.reshape(x.shape[0], -1, HD)


def call(body, us, mib, inputs, outputs, scratch=(), aliases=None):
    return pl.pallas_call(
        body,
        in_specs=[VMEM if v else HBM for _, v in inputs],
        out_specs=[VMEM if v else HBM for _, _, v in outputs],
        out_shape=[(pltpu.VMEM if v else pltpu.HBM)(s, t) for s, t, v in outputs],
        scratch_shapes=list(scratch),
        input_output_aliases=aliases or {},
        compiler_params=params(mib),
        cost_estimate=cost(us),
    )(*[in_vmem(x) if v else in_hbm(x) for x, v in inputs])


def gets(ins, outs, sem, first, pairs):
    return [
        pltpu.make_async_copy(src.at[:, first + m], dst.at[m], sem.at[i, m])
        for i, (src, dst) in enumerate(zip(ins, outs))
        for m in range(pairs)
    ]


def start(copies):
    for c in copies:
        c.start()


def wait(copies):
    for c in copies:
        c.wait()


def fetch_shapes(n, pairs, tokens):
    return [((pairs, tokens, 2, HD), jnp.bfloat16, True)] * n


def relay(arrays, first, pairs):
    n, tokens = len(arrays), arrays[0].shape[0]

    def body(*refs):
        copies = gets(refs[:n], refs[n : 2 * n], refs[-1], first, pairs)
        start(copies)
        wait(copies)

    sems = [pltpu.SemaphoreType.DMA((n, pairs))]
    outs = call(body, 1, 1, [(a, False) for a in arrays], fetch_shapes(n, pairs, tokens), sems)
    return list(map(paired, outs))


def totals(k, v, first, sums, heads, arrays, then):
    pairs, rows, _ = k.shape
    n = len(arrays) if then else 0
    held = sums is not None

    def body(k_ref, v_ref, *refs):
        refs = refs[held:]
        ins, o_ref, outs = refs[:n], refs[n], refs[n + 1 : 2 * n + 1]
        mine, sem, got = refs[2 * n + 1 :]
        copies = gets(ins, outs, got, *then) if then else []
        start(copies)

        def step(m, carry):
            s = dot(k_ref[m], by_head(v_ref[m]), ((0,), (0,)))
            mine[2 * m] = s[:, :HD]
            mine[2 * m + 1] = s[:, HD:]
            return carry

        lax.fori_loop(0, pairs, step, 0)
        out = pltpu.make_async_copy(mine, o_ref.at[pl.ds(2 * first, 2 * pairs)], sem)
        out.start()
        out.wait()
        wait(copies)

    inputs = [(k, True), (v, True)] + ([(sums, False)] if held else [])
    inputs += [(a, False) for a in arrays[:n]]
    outputs = [((heads, HD, HD), jnp.float32, False)]
    if then:
        outputs += fetch_shapes(n, then[1], rows // 2)
    scratch = [
        pltpu.VMEM((2 * pairs, HD, HD), jnp.float32),
        pltpu.SemaphoreType.DMA,
        pltpu.SemaphoreType.DMA((max(n, 1), then[1] if then else 1)),
    ]
    sums, *got = call(body, 2, 4, inputs, outputs, scratch, {2: 0} if held else None)
    return sums, list(map(paired, got))


def local(q, k, v, first, kept, arrays, then):
    pairs, rows, _ = q.shape
    blocks = rows // PAIR
    n = len(arrays) if then else 0
    every = arrays[0].shape[1]
    held = 2 if kept else 0

    def body(q_ref, k_ref, v_ref, *refs):
        refs = refs[held:]
        ins, x_ref, p_ref, outs = refs[:n], refs[n], refs[n + 1], refs[n + 2 : 2 * n + 2]
        mask, score, states, mine, sem, got = refs[2 * n + 2 :]
        copies = gets(ins, outs, got, *then) if then else []
        here = pl.ds(first, pairs)
        copies.append(pltpu.make_async_copy(q_ref, p_ref.at[here], sem.at[0]))
        start(copies)
        i = lax.broadcasted_iota(jnp.int32, (PAIR, PAIR), 0)
        j = lax.broadcasted_iota(jnp.int32, (PAIR, PAIR), 1)
        seen = (i >= j) & (lax.rem(i, 2) == lax.rem(j, 2))
        mask[...] = jnp.where(seen, 1.0, 0.0).astype(jnp.bfloat16)

        def step(m, carry):
            cuts = [pl.ds(c * PAIR, PAIR) for c in range(blocks)]
            for c, at in enumerate(cuts):
                s = dot(q_ref[m, at], k_ref[m, at], ((1,), (1,)))
                score[c] = s.astype(jnp.bfloat16) * mask[...]
            state = None
            for c, at in enumerate(cuts[:-1]):
                piece = dot(k_ref[m, at], by_head(v_ref[m, at]), ((0,), (0,)))
                state = piece if state is None else state + piece
                held = state.astype(jnp.bfloat16)
                states[c, :HD] = held[:, :HD]
                states[c, HD:] = held[:, HD:]
            for c, at in enumerate(cuts):
                x = dot(score[c], v_ref[m, at], ((1,), (0,)))
                if c > 0:
                    x += dot(by_head(q_ref[m, at]), states[c - 1], ((1,), (0,)))
                mine[m, at] = x.astype(jnp.bfloat16)
            return carry

        lax.fori_loop(0, pairs, step, 0)
        out = pltpu.make_async_copy(mine, x_ref.at[here], sem.at[1])
        out.start()
        out.wait()
        wait(copies)

    inputs = [(q, True), (k, True), (v, True)] + [(x, False) for x in kept or ()]
    inputs += [(a, False) for a in arrays[:n]]
    outputs = [((every, rows, HD), jnp.bfloat16, False)] * 2
    if then:
        outputs += fetch_shapes(n, then[1], rows // 2)
    scratch = [
        pltpu.VMEM((PAIR, PAIR), jnp.bfloat16),
        pltpu.VMEM((blocks, PAIR, PAIR), jnp.bfloat16),
        pltpu.VMEM((blocks - 1, PAIR, HD), jnp.bfloat16),
        pltpu.VMEM((pairs, rows, HD), jnp.bfloat16),
        pltpu.SemaphoreType.DMA((2,)),
        pltpu.SemaphoreType.DMA((max(n, 1), then[1] if then else 1)),
    ]
    outs = call(body, 5, 6, inputs, outputs, scratch, {3: 0, 4: 1} if kept else None)
    return outs[:2], list(map(paired, outs[2:]))


def scan(parts):
    devices, pieces = parts.shape[0], 4
    each = devices // pieces

    def body(x_ref, o_ref, mine, sem):
        def step(i, carry):
            mine[i] = carry
            return carry + x_ref[i]

        carry, copies = jnp.zeros(parts.shape[1:], jnp.float32), []
        for p in range(pieces):
            carry = lax.fori_loop(p * each, (p + 1) * each, step, carry, unroll=8)
            here = pl.ds(p * each, each)
            copies.append(pltpu.make_async_copy(mine.at[here], o_ref.at[here], sem.at[p]))
            copies[-1].start()
        wait(copies)

    scratch = [pltpu.VMEM(parts.shape, jnp.float32), pltpu.SemaphoreType.DMA((pieces,))]
    out = [(parts.shape, jnp.float32, False)]
    return call(body, 2, 4, [(parts, True)], out, scratch)[0]


def exchange(x):
    n = lax.axis_size("grp") * lax.axis_size("ctx")
    return lax.all_to_all(x.reshape(n, -1, HD), AXES, 0, 0)


def rows_of(ref, first, rows):
    return ref.at[:, pl.ds(first, rows)]


def first_part(prefix, mixed, q, rows):
    pairs = q.shape[0]

    def body(p_ref, x_ref, q_ref, held_ref, x_out, q_out, sem):
        copies = [
            pltpu.make_async_copy(rows_of(x_ref, 0, rows), x_out, sem.at[0]),
            pltpu.make_async_copy(rows_of(q_ref, 0, rows), q_out, sem.at[1]),
        ]
        start(copies)

        def step(m, carry):
            held_ref[m] = p_ref[m].astype(jnp.bfloat16)
            return carry

        lax.fori_loop(0, 2 * pairs, step, 0)
        wait(copies)

    part = ((pairs, rows, HD), jnp.bfloat16, True)
    return call(
        body,
        3,
        4,
        [(prefix, True), (mixed, False), (q, False)],
        [((2 * pairs, HD, HD), jnp.bfloat16, True), part, part],
        [pltpu.SemaphoreType.DMA((2,))],
    )


def put_out(x_ref, o_ref, sem, first):
    pairs, tokens = x_ref.shape[:2]
    here = pl.ds(first, tokens)
    return [pltpu.make_async_copy(x_ref.at[m], o_ref.at[here, m], sem.at[m]) for m in range(pairs)]


def normed(cuts, part, held, x, q, gain, mixed, every_q, ready, out):
    pairs, rows, _ = q.shape
    tokens = rows // 2
    last, begun = part == len(cuts) - 2, out is not None
    following = 0 if last else cuts[part + 2] - cuts[part + 1]
    late = ready is not None
    entries = 2 * HD * pairs

    def body(held_ref, x_ref, q_ref, g_ref, *refs):
        refs = list(refs)
        more = [] if last else [refs.pop(0), refs.pop(0)]
        done_ref = refs.pop(0) if late else None
        if begun:
            refs.pop(0)
        n_ref = refs.pop(0)
        into = [] if last else [refs.pop(0), refs.pop(0)]
        o_ref = refs.pop(0) if late else None
        kept, sem, put = refs
        copies = [
            pltpu.make_async_copy(rows_of(src, cuts[part + 1], following), dst, sem.at[i])
            for i, (src, dst) in enumerate(zip(more, into))
        ]
        if late:
            copies += put_out(done_ref, o_ref, put, cuts[part - 1] // 2)
        start(copies)
        par = parity(PAIR, HD)

        def step(c, carry):
            at = pl.ds(pl.multiple_of(c * PAIR, PAIR), PAIR)
            total = jnp.zeros((PAIR, HD), jnp.float32)
            for m in range(pairs):
                state = held_ref[2 * m : 2 * m + 2].reshape(PAIR, HD)
                y = x_ref[m, at].astype(jnp.float32) + dot(by_head(q_ref[m, at]), state, ((1,), (0,)))
                kept[m] = y
                total += y * y
            both = total + jnp.where(par == 0, pltpu.roll(total, PAIR - 1, 0), pltpu.roll(total, 1, 0))
            mean = jnp.sum(both, axis=1, keepdims=True) / entries
            scale = jnp.broadcast_to(lax.rsqrt(mean + 1e-06), (PAIR, HD))
            for m in range(pairs):
                y = (kept[m] * scale).reshape(PAIR // 8, 8, HD) * g_ref[m][None]
                n_ref[m, at] = y.reshape(PAIR, HD).astype(jnp.bfloat16)
            return carry

        lax.fori_loop(0, rows // PAIR, step, 0)
        wait(copies)

    inputs = [(held, True), (x, True), (q, True), (gain, True)]
    outputs = [((pairs, rows, HD), jnp.bfloat16, True)]
    if not last:
        piece = ((pairs, following, HD), jnp.bfloat16, True)
        inputs += [(mixed, False), (every_q, False)]
        outputs += [piece, piece]
    aliases = {}
    if late:
        inputs.append((ready, True))
        if begun:
            aliases = {len(inputs): len(outputs)}
            inputs.append((out, False))
        outputs.append(((cuts[-1] // 2, pairs, 2, HD), jnp.bfloat16, False))
    scratch = [
        pltpu.VMEM((pairs, PAIR, HD), jnp.float32),
        pltpu.SemaphoreType.DMA((2,)),
        pltpu.SemaphoreType.DMA((pairs,)),
    ]
    outs = list(call(body, 3, 6, inputs, outputs, scratch, aliases))
    ready = outs.pop(0).reshape(pairs, tokens, 2, HD)
    x, q = (None, None) if last else (outs.pop(0), outs.pop(0))
    return x, q, ready, outs.pop(0) if late else None


def relay_out(ready, out, first):
    def body(x_ref, _, o_ref, sem):
        copies = put_out(x_ref, o_ref, sem, first)
        start(copies)
        wait(copies)

    return call(
        body,
        1,
        1,
        [(ready, True), (out, False)],
        [(out.shape, out.dtype, False)],
        [pltpu.SemaphoreType.DMA((ready.shape[0],))],
        {1: 0},
    )[0]


def attend(queries, keys, values, norm_gain):
    tokens, heads, width = queries.shape
    pairs = heads // 2
    q4, k4, v4 = (x.reshape(tokens, pairs, 2, width) for x in (queries, keys, values))

    cuts = [0, 2, 6, 11, 16]
    k, v = relay([k4, v4], 0, cuts[1])
    sums = None
    for i in range(len(cuts) - 1):
        then = (cuts[i + 1], cuts[i + 2] - cuts[i + 1]) if i + 2 < len(cuts) else None
        sums, got = totals(k, v, cuts[i], sums, heads, [k4, v4], then)
        k, v = got or (None, None)
    parts = exchange(sums)
    sums = scan(parts)
    prefix = exchange(sums).reshape(heads, width, width)

    kept = None
    for half in range(2):
        step = pairs // 4
        now = relay([q4, k4, v4], 2 * half * step, step)
        for i in range(2):
            then = ((2 * half + 1) * step, step) if i == 0 else None
            kept, now = local(*now, (2 * half + i) * step, kept, [q4, k4, v4], then)
    mixed, every_q = kept

    cuts = [0, PAIR, 3 * PAIR, 5 * PAIR, 6 * PAIR]
    gain = jnp.tile(norm_gain.reshape(pairs, 2, width), (1, 4, 1))
    held, x, q = first_part(prefix, mixed, every_q, cuts[1])
    ready, out = None, None
    for part in range(len(cuts) - 1):
        x, q, ready, out = normed(cuts, part, held, x, q, gain, mixed, every_q, ready, out)
    out = relay_out(ready, out, cuts[-2] // 2)
    return out.reshape(tokens, heads, width)


def solution(mesh):
    spec = P(AXES, None, None)
    return jax.shard_map(
        attend, mesh=mesh, in_specs=(spec, spec, spec, P()), out_specs=spec, check_vma=False
    )
```

```python
import jax
import jax.numpy as jnp
from jax import lax
from jax.experimental import pallas as pl
from jax.experimental.pallas import tpu as pltpu
from jax.sharding import PartitionSpec as P


HD = 128
PAIR = 2 * HD
MIB = 1 << 20
VMEM = pl.BlockSpec(memory_space=pltpu.VMEM)
HBM = pl.BlockSpec(memory_space=pltpu.HBM)
AXES = ("grp", "ctx")


def in_vmem(x):
    return pltpu.with_memory_space_constraint(x, pltpu.VMEM)


def in_hbm(x):
    return pltpu.with_memory_space_constraint(x, pltpu.HBM)


def params(mib):
    return pltpu.CompilerParams(vmem_limit_bytes=mib * MIB)


def cost(us):
    return pl.CostEstimate(flops=int(us * 1e9), bytes_accessed=int(us * 3e6), transcendentals=0)


def dot(a, b, dims):
    return lax.dot_general(a, b, (dims, ((), ())), preferred_element_type=jnp.float32)


def parity(rows, width):
    return lax.rem(lax.broadcasted_iota(jnp.int32, (rows, width), 0), 2)


def by_head(x):
    odd = parity(16, HD).astype(jnp.bfloat16)
    tiles = x.reshape(-1, 16, HD)
    halves = [(tiles * m[None]).reshape(x.shape) for m in (1 - odd, odd)]
    return jnp.concatenate(halves, axis=1)


def paired(x):
    return x.reshape(x.shape[0], -1, HD)


def call(body, us, mib, inputs, outputs, scratch=(), aliases=None):
    return pl.pallas_call(
        body,
        in_specs=[VMEM if v else HBM for _, v in inputs],
        out_specs=[VMEM if v else HBM for _, _, v in outputs],
        out_shape=[(pltpu.VMEM if v else pltpu.HBM)(s, t) for s, t, v in outputs],
        scratch_shapes=list(scratch),
        input_output_aliases=aliases or {},
        compiler_params=params(mib),
        cost_estimate=cost(us),
    )(*[in_vmem(x) if v else in_hbm(x) for x, v in inputs])


def gets(ins, outs, sem, first, pairs):
    return [
        pltpu.make_async_copy(src.at[:, first + m], dst.at[m], sem.at[i, m])
        for i, (src, dst) in enumerate(zip(ins, outs))
        for m in range(pairs)
    ]


def start(copies):
    for c in copies:
        c.start()


def wait(copies):
    for c in copies:
        c.wait()


def fetch_shapes(n, pairs, tokens):
    return [((pairs, tokens, 2, HD), jnp.bfloat16, True)] * n


def relay(arrays, first, pairs):
    n, tokens = len(arrays), arrays[0].shape[0]

    def body(*refs):
        copies = gets(refs[:n], refs[n : 2 * n], refs[-1], first, pairs)
        start(copies)
        wait(copies)

    sems = [pltpu.SemaphoreType.DMA((n, pairs))]
    outs = call(body, 1, 1, [(a, False) for a in arrays], fetch_shapes(n, pairs, tokens), sems)
    return list(map(paired, outs))


def totals(k, v, first, sums, heads, arrays, then):
    pairs, rows, _ = k.shape
    n = len(arrays) if then else 0
    held = sums is not None

    def body(k_ref, v_ref, *refs):
        refs = refs[held:]
        ins, o_ref, outs = refs[:n], refs[n], refs[n + 1 : 2 * n + 1]
        mine, sem, got = refs[2 * n + 1 :]
        copies = gets(ins, outs, got, *then) if then else []
        start(copies)

        def step(m, carry):
            s = dot(k_ref[m], by_head(v_ref[m]), ((0,), (0,)))
            mine[2 * m] = s[:, :HD]
            mine[2 * m + 1] = s[:, HD:]
            return carry

        lax.fori_loop(0, pairs, step, 0, unroll=True)
        copies.append(pltpu.make_async_copy(mine, o_ref.at[pl.ds(2 * first, 2 * pairs)], sem))
        start(copies[-1:])
        wait(copies)

    inputs = [(k, True), (v, True)] + ([(sums, False)] if held else [])
    inputs += [(a, False) for a in arrays[:n]]
    outputs = [((heads, HD, HD), jnp.float32, False)]
    if then:
        outputs += fetch_shapes(n, then[1], rows // 2)
    scratch = [
        pltpu.VMEM((2 * pairs, HD, HD), jnp.float32),
        pltpu.SemaphoreType.DMA,
        pltpu.SemaphoreType.DMA((max(n, 1), then[1] if then else 1)),
    ]
    sums, *got = call(body, 2, 4, inputs, outputs, scratch, {2: 0} if held else None)
    return sums, list(map(paired, got))


def local(q, k, v, first, kept, arrays, then):
    pairs, rows, _ = q.shape
    blocks = rows // PAIR
    n = len(arrays) if then else 0
    every = arrays[0].shape[1]
    held = 2 if kept else 0

    def body(q_ref, k_ref, v_ref, *refs):
        refs = refs[held:]
        ins, x_ref, p_ref, outs = refs[:n], refs[n], refs[n + 1], refs[n + 2 : 2 * n + 2]
        mask, score, states, mine, sem, got = refs[2 * n + 2 :]
        copies = gets(ins, outs, got, *then) if then else []
        here = pl.ds(first, pairs)
        copies.append(pltpu.make_async_copy(q_ref, p_ref.at[here], sem.at[0]))
        start(copies)
        i = lax.broadcasted_iota(jnp.int32, (PAIR, PAIR), 0)
        j = lax.broadcasted_iota(jnp.int32, (PAIR, PAIR), 1)
        seen = (i >= j) & (lax.rem(i, 2) == lax.rem(j, 2))
        mask[...] = jnp.where(seen, 1.0, 0.0).astype(jnp.bfloat16)

        def step(m, carry):
            cuts = [pl.ds(c * PAIR, PAIR) for c in range(blocks)]
            for c, at in enumerate(cuts):
                s = dot(q_ref[m, at], k_ref[m, at], ((1,), (1,)))
                score[c] = s.astype(jnp.bfloat16) * mask[...]
            state = None
            for c, at in enumerate(cuts[:-1]):
                piece = dot(k_ref[m, at], by_head(v_ref[m, at]), ((0,), (0,)))
                state = piece if state is None else state + piece
                held = state.astype(jnp.bfloat16)
                states[c, :HD] = held[:, :HD]
                states[c, HD:] = held[:, HD:]
            for c, at in enumerate(cuts):
                x = dot(score[c], v_ref[m, at], ((1,), (0,)))
                if c > 0:
                    x += dot(by_head(q_ref[m, at]), states[c - 1], ((1,), (0,)))
                mine[m, at] = x.astype(jnp.bfloat16)
            return carry

        lax.fori_loop(0, pairs, step, 0)
        out = pltpu.make_async_copy(mine, x_ref.at[here], sem.at[1])
        out.start()
        out.wait()
        wait(copies)

    inputs = [(q, True), (k, True), (v, True)] + [(x, False) for x in kept or ()]
    inputs += [(a, False) for a in arrays[:n]]
    outputs = [((every, rows, HD), jnp.bfloat16, False)] * 2
    if then:
        outputs += fetch_shapes(n, then[1], rows // 2)
    scratch = [
        pltpu.VMEM((PAIR, PAIR), jnp.bfloat16),
        pltpu.VMEM((blocks, PAIR, PAIR), jnp.bfloat16),
        pltpu.VMEM((blocks - 1, PAIR, HD), jnp.bfloat16),
        pltpu.VMEM((pairs, rows, HD), jnp.bfloat16),
        pltpu.SemaphoreType.DMA((2,)),
        pltpu.SemaphoreType.DMA((max(n, 1), then[1] if then else 1)),
    ]
    outs = call(body, 5, 6, inputs, outputs, scratch, {3: 0, 4: 1} if kept else None)
    return outs[:2], list(map(paired, outs[2:]))


def scan(parts):
    devices, pieces = parts.shape[0], 4
    each = devices // pieces

    def body(x_ref, o_ref, mine, sem):
        def step(i, carry):
            mine[i] = carry
            return carry + x_ref[i]

        carry, copies = jnp.zeros(parts.shape[1:], jnp.float32), []
        for p in range(pieces):
            carry = lax.fori_loop(p * each, (p + 1) * each, step, carry, unroll=8)
            here = pl.ds(p * each, each)
            copies.append(pltpu.make_async_copy(mine.at[here], o_ref.at[here], sem.at[p]))
            copies[-1].start()
        wait(copies)

    scratch = [pltpu.VMEM(parts.shape, jnp.float32), pltpu.SemaphoreType.DMA((pieces,))]
    out = [(parts.shape, jnp.float32, False)]
    return call(body, 2, 4, [(parts, True)], out, scratch)[0]


def exchange(x):
    n = lax.axis_size("grp") * lax.axis_size("ctx")
    return lax.all_to_all(x.reshape(n, -1, HD), AXES, 0, 0)


def rows_of(ref, first, rows):
    return ref.at[:, pl.ds(first, rows)]


def put_out(x_ref, o_ref, sem, first):
    pairs, tokens = x_ref.shape[:2]
    here = pl.ds(first, tokens)
    return [pltpu.make_async_copy(x_ref.at[m], o_ref.at[here, m], sem.at[m]) for m in range(pairs)]


def normed(cuts, part, held, x, q, gain, mixed, every_q, ready, out):
    pairs, rows = every_q.shape[0], cuts[part + 1] - cuts[part]
    opening = part == 0
    last, begun = part == len(cuts) - 2, out is not None
    following = 0 if last else cuts[part + 2] - cuts[part + 1]
    late = ready is not None
    entries = 2 * HD * pairs

    def body(held_ref, g_ref, *refs):
        refs = list(refs)
        x_ref, q_ref = (None, None) if opening else (refs.pop(0), refs.pop(0))
        more = [] if last else [refs.pop(0), refs.pop(0)]
        done_ref = refs.pop(0) if late else None
        if begun:
            refs.pop(0)
        n_ref = refs.pop(0)
        into = [] if last else [refs.pop(0), refs.pop(0)]
        o_ref = refs.pop(0) if late else None
        wide = held_ref
        if opening:
            held_ref, kept, sem, put, x_ref, q_ref, own = refs
            mine = [
                pltpu.make_async_copy(rows_of(src, 0, rows), dst, own.at[i])
                for i, (src, dst) in enumerate(zip(more, (x_ref, q_ref)))
            ]
            start(mine)
        else:
            kept, sem, put = refs
        copies = [
            pltpu.make_async_copy(rows_of(src, cuts[part + 1], following), dst, sem.at[i])
            for i, (src, dst) in enumerate(zip(more, into))
        ]
        if late:
            copies += put_out(done_ref, o_ref, put, cuts[part - 1] // 2)
        start(copies)
        if opening:

            def narrow(m, carry):
                held_ref[m] = wide[m].astype(jnp.bfloat16)
                return carry

            lax.fori_loop(0, 2 * pairs, narrow, 0, unroll=4)
            wait(mine)
        par = parity(PAIR, HD)

        def step(c, carry):
            at = pl.ds(pl.multiple_of(c * PAIR, PAIR), PAIR)
            total = jnp.zeros((PAIR, HD), jnp.float32)
            for m in range(pairs):
                state = held_ref[2 * m : 2 * m + 2].reshape(PAIR, HD)
                y = x_ref[m, at].astype(jnp.float32) + dot(by_head(q_ref[m, at]), state, ((1,), (0,)))
                kept[m] = y
                total += y * y
            both = total + jnp.where(par == 0, pltpu.roll(total, PAIR - 1, 0), pltpu.roll(total, 1, 0))
            mean = jnp.sum(both, axis=1, keepdims=True) / entries
            scale = jnp.broadcast_to(lax.rsqrt(mean + 1e-06), (PAIR, HD))
            for m in range(pairs):
                y = (kept[m] * scale).reshape(PAIR // 8, 8, HD) * g_ref[m][None]
                n_ref[m, at] = y.reshape(PAIR, HD).astype(jnp.bfloat16)
            return carry

        lax.fori_loop(0, rows // PAIR, step, 0)
        wait(copies)

    inputs = [(held, True), (gain, True)] + ([] if opening else [(x, True), (q, True)])
    outputs = [((pairs, rows, HD), jnp.bfloat16, True)]
    if not last:
        piece = ((pairs, following, HD), jnp.bfloat16, True)
        inputs += [(mixed, False), (every_q, False)]
        outputs += [piece, piece]
    aliases = {}
    if late:
        inputs.append((ready, True))
        if begun:
            aliases = {len(inputs): len(outputs)}
            inputs.append((out, False))
        outputs.append(((cuts[-1] // 2, pairs, 2, HD), jnp.bfloat16, False))
    scratch = [
        pltpu.VMEM((pairs, PAIR, HD), jnp.float32),
        pltpu.SemaphoreType.DMA((2,)),
        pltpu.SemaphoreType.DMA((pairs,)),
    ]
    if opening:
        outputs.append(((2 * pairs, HD, HD), jnp.bfloat16, True))
        scratch += [pltpu.VMEM((pairs, rows, HD), jnp.bfloat16)] * 2 + [pltpu.SemaphoreType.DMA((2,))]
    outs = list(call(body, 3, 8, inputs, outputs, scratch, aliases))
    ready = outs.pop(0).reshape(pairs, rows // 2, 2, HD)
    x, q = (None, None) if last else (outs.pop(0), outs.pop(0))
    out = outs.pop(0) if late else None
    return outs.pop(0) if opening else held, x, q, ready, out


def relay_out(ready, out, first):
    def body(x_ref, _, o_ref, sem):
        copies = put_out(x_ref, o_ref, sem, first)
        start(copies)
        wait(copies)

    return call(
        body,
        1,
        1,
        [(ready, True), (out, False)],
        [(out.shape, out.dtype, False)],
        [pltpu.SemaphoreType.DMA((ready.shape[0],))],
        {1: 0},
    )[0]


def attend(queries, keys, values, norm_gain):
    tokens, heads, width = queries.shape
    pairs = heads // 2
    q4, k4, v4 = (x.reshape(tokens, pairs, 2, width) for x in (queries, keys, values))

    cuts = [0, 7, 14, 16]
    k, v = relay([k4, v4], 0, cuts[1])
    sums = None
    for i in range(len(cuts) - 1):
        then = (cuts[i + 1], cuts[i + 2] - cuts[i + 1]) if i + 2 < len(cuts) else None
        sums, got = totals(k, v, cuts[i], sums, heads, [k4, v4], then)
        k, v = got or (None, None)
    parts = exchange(sums)
    sums = scan(parts)
    prefix = exchange(sums).reshape(heads, width, width)

    kept = None
    for half in range(2):
        step = pairs // 4
        now = relay([q4, k4, v4], 2 * half * step, step)
        for i in range(2):
            then = ((2 * half + 1) * step, step) if i == 0 else None
            kept, now = local(*now, (2 * half + i) * step, kept, [q4, k4, v4], then)
    mixed, every_q = kept

    cuts = [0, PAIR, 3 * PAIR, 5 * PAIR, 6 * PAIR]
    gain = jnp.tile(norm_gain.reshape(pairs, 2, width), (1, 4, 1))
    held, x, q, ready, out = prefix, None, None, None, None
    for part in range(len(cuts) - 1):
        held, x, q, ready, out = normed(cuts, part, held, x, q, gain, mixed, every_q, ready, out)
    out = relay_out(ready, out, cuts[-2] // 2)
    return out.reshape(tokens, heads, width)


def solution(mesh):
    spec = P(AXES, None, None)
    return jax.shard_map(
        attend, mesh=mesh, in_specs=(spec, spec, spec, P()), out_specs=spec, check_vma=False
    )
```

```python
import jax
import jax.numpy as jnp
from jax import lax
from jax.experimental import pallas as pl
from jax.experimental.pallas import tpu as pltpu
from jax.sharding import PartitionSpec as P


HD = 128
PAIR = 2 * HD
MIB = 1 << 20
VMEM = pl.BlockSpec(memory_space=pltpu.VMEM)
HBM = pl.BlockSpec(memory_space=pltpu.HBM)
AXES = ("grp", "ctx")


def in_vmem(x):
    return pltpu.with_memory_space_constraint(x, pltpu.VMEM)


def in_hbm(x):
    return pltpu.with_memory_space_constraint(x, pltpu.HBM)


def params(mib):
    return pltpu.CompilerParams(vmem_limit_bytes=mib * MIB)


def cost(us):
    return pl.CostEstimate(flops=int(us * 1e9), bytes_accessed=int(us * 3e6), transcendentals=0)


def dot(a, b, dims):
    return lax.dot_general(a, b, (dims, ((), ())), preferred_element_type=jnp.float32)


def parity(rows, width):
    return lax.rem(lax.broadcasted_iota(jnp.int32, (rows, width), 0), 2)


def by_head(x):
    odd = parity(16, HD).astype(jnp.bfloat16)
    tiles = x.reshape(-1, 16, HD)
    halves = [(tiles * m[None]).reshape(x.shape) for m in (1 - odd, odd)]
    return jnp.concatenate(halves, axis=1)


def paired(x):
    return x.reshape(x.shape[0], -1, HD)


def call(body, us, mib, inputs, outputs, scratch=(), aliases=None):
    return pl.pallas_call(
        body,
        in_specs=[VMEM if v else HBM for _, v in inputs],
        out_specs=[VMEM if v else HBM for _, _, v in outputs],
        out_shape=[(pltpu.VMEM if v else pltpu.HBM)(s, t) for s, t, v in outputs],
        scratch_shapes=list(scratch),
        input_output_aliases=aliases or {},
        compiler_params=params(mib),
        cost_estimate=cost(us),
    )(*[in_vmem(x) if v else in_hbm(x) for x, v in inputs])


def gets(ins, outs, sem, first, pairs):
    return [
        pltpu.make_async_copy(src.at[:, first + m], dst.at[m], sem.at[i, m])
        for i, (src, dst) in enumerate(zip(ins, outs))
        for m in range(pairs)
    ]


def start(copies):
    for c in copies:
        c.start()


def wait(copies):
    for c in copies:
        c.wait()


def fetch_shapes(n, pairs, tokens):
    return [((pairs, tokens, 2, HD), jnp.bfloat16, True)] * n


def relay(arrays, first, pairs):
    n, tokens = len(arrays), arrays[0].shape[0]

    def body(*refs):
        copies = gets(refs[:n], refs[n : 2 * n], refs[-1], first, pairs)
        start(copies)
        wait(copies)

    sems = [pltpu.SemaphoreType.DMA((n, pairs))]
    outs = call(body, 1, 1, [(a, False) for a in arrays], fetch_shapes(n, pairs, tokens), sems)
    return list(map(paired, outs))


def totals(k, v, first, sums, ready, heads, arrays, then):
    pairs, rows, _ = k.shape
    n = len(arrays) if then else 0
    late, held = ready is not None, sums is not None

    def body(k_ref, v_ref, *refs):
        refs = list(refs)
        ins = [refs.pop(0) for _ in range(n)]
        ready_ref = refs.pop(0) if late else None
        if held:
            refs.pop(0)
        mine = refs.pop(0) if then else None
        o_ref = refs.pop(0) if late else None
        outs = [refs.pop(0) for _ in range(n)]
        sem, got = refs[:2]
        mine = mine if then else refs[2]
        copies = gets(ins, outs, got, *then) if then else []
        if late:
            before = ready_ref.shape[0]
            here = o_ref.at[pl.ds(2 * first - before, before)]
            copies.append(pltpu.make_async_copy(ready_ref, here, sem.at[0]))
        start(copies)

        def step(m, carry):
            s = dot(k_ref[m], by_head(v_ref[m]), ((0,), (0,)))
            mine[2 * m] = s[:, :HD]
            mine[2 * m + 1] = s[:, HD:]
            return carry

        lax.fori_loop(0, pairs, step, 0, unroll=True)
        if not then:
            here = o_ref.at[pl.ds(2 * first, 2 * pairs)]
            copies.append(pltpu.make_async_copy(mine, here, sem.at[1]))
            start(copies[-1:])
        wait(copies)

    inputs = [(k, True), (v, True)] + [(a, False) for a in arrays[:n]]
    piece, outputs, aliases = ((2 * pairs, HD, HD), jnp.float32), [], {}
    scratch = [
        pltpu.SemaphoreType.DMA((2,)),
        pltpu.SemaphoreType.DMA((max(n, 1), then[1] if then else 1)),
    ]
    if then:
        outputs.append((*piece, True))
    else:
        scratch.append(pltpu.VMEM(*piece))
    if late:
        inputs.append((ready, True))
        if held:
            aliases = {len(inputs): len(outputs)}
            inputs.append((sums, False))
        outputs.append(((heads, HD, HD), jnp.float32, False))
    outputs += fetch_shapes(n, then[1] if then else 0, rows // 2)
    outs = list(call(body, 2, 4, inputs, outputs, scratch, aliases))
    ready = outs.pop(0) if then else None
    sums = outs.pop(0) if late else None
    return sums, ready, list(map(paired, outs))


def local(q, k, v, first, kept, arrays, then):
    pairs, rows, _ = q.shape
    blocks = rows // PAIR
    n = len(arrays) if then else 0
    every = arrays[0].shape[1]
    held = 2 if kept else 0

    def body(q_ref, k_ref, v_ref, *refs):
        refs = refs[held:]
        ins, x_ref, p_ref, outs = refs[:n], refs[n], refs[n + 1], refs[n + 2 : 2 * n + 2]
        mask, score, states, mine, sem, got = refs[2 * n + 2 :]
        copies = gets(ins, outs, got, *then) if then else []
        here = pl.ds(first, pairs)
        copies.append(pltpu.make_async_copy(q_ref, p_ref.at[here], sem.at[0]))
        start(copies)
        i = lax.broadcasted_iota(jnp.int32, (PAIR, PAIR), 0)
        j = lax.broadcasted_iota(jnp.int32, (PAIR, PAIR), 1)
        seen = (i >= j) & (lax.rem(i, 2) == lax.rem(j, 2))
        mask[...] = jnp.where(seen, 1.0, 0.0).astype(jnp.bfloat16)

        def step(m, carry):
            cuts = [pl.ds(c * PAIR, PAIR) for c in range(blocks)]
            for c, at in enumerate(cuts):
                s = dot(q_ref[m, at], k_ref[m, at], ((1,), (1,)))
                score[c] = s.astype(jnp.bfloat16) * mask[...]
            state = None
            for c, at in enumerate(cuts[:-1]):
                piece = dot(k_ref[m, at], by_head(v_ref[m, at]), ((0,), (0,)))
                state = piece if state is None else state + piece
                held = state.astype(jnp.bfloat16)
                states[c, :HD] = held[:, :HD]
                states[c, HD:] = held[:, HD:]
            for c, at in enumerate(cuts):
                x = dot(score[c], v_ref[m, at], ((1,), (0,)))
                if c > 0:
                    x += dot(by_head(q_ref[m, at]), states[c - 1], ((1,), (0,)))
                mine[m, at] = x.astype(jnp.bfloat16)
            return carry

        lax.fori_loop(0, pairs, step, 0)
        out = pltpu.make_async_copy(mine, x_ref.at[here], sem.at[1])
        out.start()
        out.wait()
        wait(copies)

    inputs = [(q, True), (k, True), (v, True)] + [(x, False) for x in kept or ()]
    inputs += [(a, False) for a in arrays[:n]]
    outputs = [((every, rows, HD), jnp.bfloat16, False)] * 2
    if then:
        outputs += fetch_shapes(n, then[1], rows // 2)
    scratch = [
        pltpu.VMEM((PAIR, PAIR), jnp.bfloat16),
        pltpu.VMEM((blocks, PAIR, PAIR), jnp.bfloat16),
        pltpu.VMEM((blocks - 1, PAIR, HD), jnp.bfloat16),
        pltpu.VMEM((pairs, rows, HD), jnp.bfloat16),
        pltpu.SemaphoreType.DMA((2,)),
        pltpu.SemaphoreType.DMA((max(n, 1), then[1] if then else 1)),
    ]
    outs = call(body, 5, 6, inputs, outputs, scratch, {3: 0, 4: 1} if kept else None)
    return outs[:2], list(map(paired, outs[2:]))


def scan(parts):
    devices, pieces = parts.shape[0], 4
    each = devices // pieces

    def body(x_ref, o_ref, mine, sem):
        def step(i, carry):
            mine[i] = carry
            return carry + x_ref[i]

        carry, copies = jnp.zeros(parts.shape[1:], jnp.float32), []
        for p in range(pieces):
            carry = lax.fori_loop(p * each, (p + 1) * each, step, carry, unroll=8)
            here = pl.ds(p * each, each)
            copies.append(pltpu.make_async_copy(mine.at[here], o_ref.at[here], sem.at[p]))
            copies[-1].start()
        wait(copies)

    scratch = [pltpu.VMEM(parts.shape, jnp.float32), pltpu.SemaphoreType.DMA((pieces,))]
    out = [(parts.shape, jnp.float32, False)]
    return call(body, 2, 4, [(parts, True)], out, scratch)[0]


def exchange(x):
    n = lax.axis_size("grp") * lax.axis_size("ctx")
    return lax.all_to_all(x.reshape(n, -1, HD), AXES, 0, 0)


def rows_of(ref, first, rows):
    return ref.at[:, pl.ds(first, rows)]


def put_out(x_ref, o_ref, sem, first):
    pairs, tokens = x_ref.shape[:2]
    here = pl.ds(first, tokens)
    return [pltpu.make_async_copy(x_ref.at[m], o_ref.at[here, m], sem.at[m]) for m in range(pairs)]


def normed(cuts, part, held, x, q, gain, mixed, every_q, ready, out):
    pairs, rows = every_q.shape[0], cuts[part + 1] - cuts[part]
    opening = part == 0
    last, begun = part == len(cuts) - 2, out is not None
    following = 0 if last else cuts[part + 2] - cuts[part + 1]
    late = ready is not None
    entries = 2 * HD * pairs

    def body(held_ref, g_ref, *refs):
        refs = list(refs)
        x_ref, q_ref = (None, None) if opening else (refs.pop(0), refs.pop(0))
        more = [] if last else [refs.pop(0), refs.pop(0)]
        done_ref = refs.pop(0) if late else None
        if begun:
            refs.pop(0)
        n_ref = refs.pop(0)
        into = [] if last else [refs.pop(0), refs.pop(0)]
        o_ref = refs.pop(0) if late else None
        wide = held_ref
        if opening:
            held_ref, kept, sem, put, x_ref, q_ref, own = refs
            mine = [
                pltpu.make_async_copy(rows_of(src, 0, rows), dst, own.at[i])
                for i, (src, dst) in enumerate(zip(more, (x_ref, q_ref)))
            ]
            start(mine)
        else:
            kept, sem, put = refs
        copies = [
            pltpu.make_async_copy(rows_of(src, cuts[part + 1], following), dst, sem.at[i])
            for i, (src, dst) in enumerate(zip(more, into))
        ]
        if late:
            copies += put_out(done_ref, o_ref, put, cuts[part - 1] // 2)
        start(copies)
        if opening:

            def narrow(m, carry):
                held_ref[m] = wide[m].astype(jnp.bfloat16)
                return carry

            lax.fori_loop(0, 2 * pairs, narrow, 0, unroll=4)
            wait(mine)
        par = parity(PAIR, HD)

        def step(c, carry):
            at = pl.ds(pl.multiple_of(c * PAIR, PAIR), PAIR)
            total = jnp.zeros((PAIR, HD), jnp.float32)
            for m in range(pairs):
                state = held_ref[2 * m : 2 * m + 2].reshape(PAIR, HD)
                y = x_ref[m, at].astype(jnp.float32) + dot(by_head(q_ref[m, at]), state, ((1,), (0,)))
                kept[m] = y
                total += y * y
            both = total + jnp.where(par == 0, pltpu.roll(total, PAIR - 1, 0), pltpu.roll(total, 1, 0))
            mean = jnp.sum(both, axis=1, keepdims=True) / entries
            scale = jnp.broadcast_to(lax.rsqrt(mean + 1e-06), (PAIR, HD))
            for m in range(pairs):
                y = (kept[m] * scale).reshape(PAIR // 8, 8, HD) * g_ref[m][None]
                n_ref[m, at] = y.reshape(PAIR, HD).astype(jnp.bfloat16)
            return carry

        lax.fori_loop(0, rows // PAIR, step, 0)
        wait(copies)

    inputs = [(held, True), (gain, True)] + ([] if opening else [(x, True), (q, True)])
    outputs = [((pairs, rows, HD), jnp.bfloat16, True)]
    if not last:
        piece = ((pairs, following, HD), jnp.bfloat16, True)
        inputs += [(mixed, False), (every_q, False)]
        outputs += [piece, piece]
    aliases = {}
    if late:
        inputs.append((ready, True))
        if begun:
            aliases = {len(inputs): len(outputs)}
            inputs.append((out, False))
        outputs.append(((cuts[-1] // 2, pairs, 2, HD), jnp.bfloat16, False))
    scratch = [
        pltpu.VMEM((pairs, PAIR, HD), jnp.float32),
        pltpu.SemaphoreType.DMA((2,)),
        pltpu.SemaphoreType.DMA((pairs,)),
    ]
    if opening:
        outputs.append(((2 * pairs, HD, HD), jnp.bfloat16, True))
        scratch += [pltpu.VMEM((pairs, rows, HD), jnp.bfloat16)] * 2 + [pltpu.SemaphoreType.DMA((2,))]
    outs = list(call(body, 3, 8, inputs, outputs, scratch, aliases))
    ready = outs.pop(0).reshape(pairs, rows // 2, 2, HD)
    x, q = (None, None) if last else (outs.pop(0), outs.pop(0))
    out = outs.pop(0) if late else None
    return outs.pop(0) if opening else held, x, q, ready, out


def relay_out(ready, out, first):
    def body(x_ref, _, o_ref, sem):
        copies = put_out(x_ref, o_ref, sem, first)
        start(copies)
        wait(copies)

    return call(
        body,
        1,
        1,
        [(ready, True), (out, False)],
        [(out.shape, out.dtype, False)],
        [pltpu.SemaphoreType.DMA((ready.shape[0],))],
        {1: 0},
    )[0]


def attend(queries, keys, values, norm_gain):
    tokens, heads, width = queries.shape
    pairs = heads // 2
    q4, k4, v4 = (x.reshape(tokens, pairs, 2, width) for x in (queries, keys, values))

    cuts = [0, 7, 14, 16]
    k, v = relay([k4, v4], 0, cuts[1])
    sums, ready = None, None
    for i in range(len(cuts) - 1):
        then = (cuts[i + 1], cuts[i + 2] - cuts[i + 1]) if i + 2 < len(cuts) else None
        sums, ready, got = totals(k, v, cuts[i], sums, ready, heads, [k4, v4], then)
        k, v = got or (None, None)
    parts = exchange(sums)
    sums = scan(parts)
    prefix = exchange(sums).reshape(heads, width, width)

    kept = None
    for half in range(2):
        step = pairs // 4
        now = relay([q4, k4, v4], 2 * half * step, step)
        for i in range(2):
            then = ((2 * half + 1) * step, step) if i == 0 else None
            kept, now = local(*now, (2 * half + i) * step, kept, [q4, k4, v4], then)
    mixed, every_q = kept

    cuts = [0, PAIR, 3 * PAIR, 5 * PAIR, 6 * PAIR]
    gain = jnp.tile(norm_gain.reshape(pairs, 2, width), (1, 4, 1))
    held, x, q, ready, out = prefix, None, None, None, None
    for part in range(len(cuts) - 1):
        held, x, q, ready, out = normed(cuts, part, held, x, q, gain, mixed, every_q, ready, out)
    out = relay_out(ready, out, cuts[-2] // 2)
    return out.reshape(tokens, heads, width)


def solution(mesh):
    spec = P(AXES, None, None)
    return jax.shard_map(
        attend, mesh=mesh, in_specs=(spec, spec, spec, P()), out_specs=spec, check_vma=False
    )
```
